256 devices in a mesh: ctx: 32 (over x_lo, z, core), tp: 8 (over x_hi, y).
Axes of the slice: x: 4 (x_hi: 2, x_lo: 2; x = x_hi * 2 + x_lo), y: 4, z: 8, core: 2. Of those that a mesh axis runs over, the one named last changes fastest.
Arguments:
- patches: bfloat16 [4, 4096, 6144], P(None, 'ctx', 'tp'), may hold values from -24 to 24
- ln_gain: float32 [6144], replicated, may hold values from 0.25 to 1.75
- w_qkv: bfloat16 [6144, 3, 24, 128], P('ctx', None, 'tp'), may hold values from -0.078125 to 0.078125
- query_gain: float32 [24, 128], P('tp'), may hold values from 0.5 to 8
- key_gain: float32 [24, 128], P('tp'), may hold values from 0.5 to 8
Outputs:
- attended: bfloat16 [4, 4096, 24, 128], P(None, 'ctx', 'tp')
The draws below stay inside these ranges and needn't reach their ends.
All inputs are finite; a program needn't handle non-finite values.
Results may differ from the reference program's by a relative error of at most 0.007.
The reference program's roundings to bfloat16 on the way (of `normed`, `values` and `probs`) count: a program that leaves them out, or rounds other values in their place, can miss the bound.
Values may be sent and summed in bfloat16 or wider, within the bound.
No kernel may reach another device: no remote copies, remote signals or barrier semaphores. Data moves between devices by JAX's collectives and lax.ppermute only.
A program may use at most 192 MiB of HBM per device.

```python
import jax
import jax.numpy as jnp
from jax import lax

D = 6144
HEADS = 24
HD = 128
CROPS = 4
SEQ = 4096


def draw_patches(key, part):
    key_noise = jax.random.fold_in(key, 11)
    key_feature = jax.random.fold_in(key, 12)
    noise = jax.random.normal(key_noise, (CROPS, SEQ, D), jnp.float32)
    feature_scale = jnp.exp(jax.random.uniform(key_feature, (D,), jnp.float32, jnp.log(0.5), jnp.log(2.0)))
    drawn = noise * feature_scale
    return jnp.clip(drawn, -24.0, 24.0).astype(jnp.bfloat16)


def gain_draw(key):
    key_entry = jax.random.fold_in(key, 21)
    return jnp.exp(jax.random.uniform(key_entry, (HEADS, HD), jnp.float32, jnp.log(1.2), jnp.log(2.5)))


def draw_query_gain(key, part):
    return gain_draw(jax.random.fold_in(key, 31))


def draw_key_gain(key, part):
    return gain_draw(jax.random.fold_in(key, 32))


def shard_levels(stream_key, extent, shards, low, top_value):
    loudness, own = 1.0, jax.random.fold_in(stream_key, 6)
    for position, parts in shards:
        heights = jnp.exp(jax.random.uniform(jax.random.fold_in(own, position), (parts,), jnp.float32, low / len(shards), top_value / len(shards)))
        loudness = loudness * jnp.repeat(heights, extent[position] // parts).reshape([-1 if axis == position else 1 for axis in range(len(extent))])
    return loudness


def bell_draw(own_key, extent, deviation, limit, split=(), held_as=jnp.bfloat16):
    entries = jax.random.normal(own_key, extent, jnp.float32) * deviation
    if len(split) > 0:
        entries = shard_levels(own_key, extent, split, -0.22, 0.18) * entries
    return jnp.clip(entries, min=-limit, max=limit).astype(held_as)


def setup_inputs(seed: int = 0) -> dict:
    key_of = jax.random.split(jax.random.key(seed), 6)
    patches = draw_patches(jax.random.fold_in(key_of[5], 71), 0)
    ln_gain = jnp.clip(1.0 + 0.15 * jax.random.normal(key_of[1], (D,), jnp.float32), 0.25, 1.75)
    w_qkv = bell_draw(key_of[2], (D, 3, HEADS, HD), D ** -0.5, 0.078125, ((0, 32), (2, 8)))
    query_gain = draw_query_gain(jax.random.fold_in(key_of[5], 71), 0)
    key_gain = draw_key_gain(jax.random.fold_in(key_of[5], 71), 0)
    return {"patches": patches, "ln_gain": ln_gain, "w_qkv": w_qkv, "query_gain": query_gain, "key_gain": key_gain}


def layer_norm(values_in, gain):
    center = lax.optimization_barrier(jnp.mean(values_in, axis=-1, keepdims=True))
    spread = lax.optimization_barrier(jnp.mean(values_in * values_in, axis=-1, keepdims=True)) - center * center
    return (values_in - center) * lax.rsqrt(spread + 1e-06) * gain

def attend(triple):
    query_head, key_head, value_head = triple
    scores = jnp.dot(query_head, key_head.T, preferred_element_type=jnp.float32) / jnp.sqrt(jnp.float32(HD))
    expd = jnp.exp(scores - lax.optimization_barrier(jnp.max(scores, axis=-1, keepdims=True)))
    totals = lax.optimization_barrier(jnp.sum(expd, axis=-1, keepdims=True))
    probs = expd.astype(jnp.bfloat16)
    summed = jnp.dot(probs, value_head, preferred_element_type=jnp.float32)
    return (summed / totals).astype(jnp.bfloat16)

def reference(patches, ln_gain, w_qkv, query_gain, key_gain):
    normed = layer_norm(patches.astype(jnp.float32), ln_gain).astype(jnp.bfloat16)
    projected = jnp.dot(normed.reshape(CROPS * SEQ, D), w_qkv.reshape(D, 3 * HEADS * HD), preferred_element_type=jnp.float32)
    projected = projected.reshape(CROPS, SEQ, 3, HEADS, HD)
    queries = layer_norm(projected[:, :, 0], query_gain).astype(jnp.bfloat16)
    keys = layer_norm(projected[:, :, 1], key_gain).astype(jnp.bfloat16)
    values = projected[:, :, 2].astype(jnp.bfloat16)

    def heads_first(array):
        return jnp.transpose(array, (0, 2, 1, 3)).reshape(CROPS * HEADS, SEQ, HD)
    result = lax.map(attend, (heads_first(queries), heads_first(keys), heads_first(values)))
    return jnp.transpose(result.reshape(CROPS, HEADS, SEQ, HD), (0, 2, 1, 3))
```

```python
import jax
import jax.numpy as jnp
from jax import lax
from jax.experimental import pallas as pl
from jax.experimental.pallas import tpu as pltpu
from jax.sharding import Mesh, PartitionSpec as P

TP = 8
KB = 768
SUB = 192
HD = 128
SWAP = [(0, 1), (1, 0)]
VMEM_LIMIT = 58 * 1024 * 1024
ANY = pl.BlockSpec(memory_space=pl.ANY)


def ring(n, shift):
    return [(i, (i + shift) % n) for i in range(n)]


def features_index(xh, y, a, b):
    return lax.rem(xh + a, 2) * 4 + lax.rem(y + b, 4)


def norm_kernel(*refs):
    pieces, gain_ref, out_ref, held, sems = refs[:12], refs[12], refs[13], refs[14], refs[15]
    xh, y = lax.axis_index("xh"), lax.axis_index("y")
    row0 = 0
    copies = []
    for chunk in range(2):
        c0, c1, f, b, g, h = pieces[6 * chunk : 6 * chunk + 6]
        rows = c0.shape[0]
        plan = (
            (c0, 0, 0),
            (c1, 1, 0),
            (f.at[0], 0, 3),
            (f.at[1], 1, 3),
            (b.at[0], 0, 1),
            (b.at[1], 1, 1),
            (g, 0, 2),
            (h, 1, 2),
        )
        for src, dx, dy in plan:
            t = features_index(xh, y, dx, dy)
            copy = pltpu.make_async_copy(
                src, held.at[t, pl.ds(row0, rows), :], sems.at[len(copies)]
            )
            copy.start()
            copies.append(copy)
        row0 += rows
    tile = 16

    def rows_step(i, carry):
        r = pl.multiple_of(i * tile, tile)
        total = jnp.zeros((tile, 1), jnp.float32)
        square = jnp.zeros((tile, 1), jnp.float32)
        part = jnp.zeros((tile, 128), jnp.float32)
        part2 = jnp.zeros((tile, 128), jnp.float32)
        for t in range(TP):
            block = held[t, pl.ds(r, tile), :].astype(jnp.float32)
            for j in range(KB // 128):
                piece = block[:, j * 128 : (j + 1) * 128]
                part = part + piece
                part2 = part2 + piece * piece
        total = jnp.sum(part, axis=-1, keepdims=True)
        square = jnp.sum(part2, axis=-1, keepdims=True)
        center = total * (1.0 / (TP * KB))
        spread = square * (1.0 / (TP * KB)) - center * center
        scale = lax.rsqrt(spread + 1e-06)
        for t in range(TP):
            block = held[t, pl.ds(r, tile), :].astype(jnp.float32)
            out_ref[t, pl.ds(r, tile), :] = (
                (block - center) * scale * gain_ref[t : t + 1, :]
            ).astype(jnp.bfloat16)
        return carry

    split = pieces[0].shape[0] // tile
    for copy in copies[:8]:
        copy.wait()
    lax.fori_loop(0, split, rows_step, 0)
    for copy in copies[8:]:
        copy.wait()
    lax.fori_loop(split, row0 // tile, rows_step, 0)


def norm_rows(pieces, gain):
    return pl.pallas_call(
        norm_kernel,
        out_shape=jax.ShapeDtypeStruct((TP, 512, KB), jnp.bfloat16),
        in_specs=[ANY] * 12 + [pl.BlockSpec(memory_space=pltpu.VMEM)],
        out_specs=pl.BlockSpec(memory_space=pltpu.VMEM),
        scratch_shapes=[
            pltpu.VMEM((TP, 512, KB), jnp.bfloat16),
            pltpu.SemaphoreType.DMA((16,)),
        ],
        compiler_params=pltpu.CompilerParams(vmem_limit_bytes=VMEM_LIMIT),
    )(*pieces, gain)


def head_norm(values_in, gain):
    center = jnp.mean(values_in, axis=-1, keepdims=True)
    spread = jnp.mean(values_in * values_in, axis=-1, keepdims=True) - center * center
    return (values_in - center) * lax.rsqrt(spread + 1e-06) * gain


def load_weight(parts, held, col, sems, first):
    xl, core = lax.axis_index("xl"), lax.axis_index("core")
    copies = []
    for dc, dx, piece in parts:
        for z in range(8):
            t = lax.rem(xl + dx, 2) * 4 + z // 2
            copies.append(
                pltpu.make_async_copy(
                    piece.at[z],
                    held.at[t, z % 2, lax.rem(core + dc, 2), :, pl.ds(col, 384)],
                    sems.at[first + len(copies)],
                )
            )
    return copies


def project_kv_kernel(x_ref, *refs):
    k_parts, v_parts, gain_ref, kv_ref, held, total, sems = (
        refs[:4], refs[4:6], refs[6], refs[7], refs[8], refs[9], refs[10]
    )
    own = [(0, 0, k_parts[0]), (0, 1, k_parts[1]), (1, 0, k_parts[2]), (1, 1, k_parts[3])]
    copies = load_weight(own, held, 0, sems, 0)
    both = [(dc, dx, v_parts[dc].at[dx]) for dc in range(2) for dx in range(2)]
    copies += load_weight(both, held, 384, sems, 32)
    for copy in copies:
        copy.start()
    for copy in copies:
        copy.wait()
    total[...] = jnp.zeros_like(total)

    def step(t, carry):
        weight = held[t].reshape(KB, 768)
        total[...] += jnp.dot(x_ref[t], weight, preferred_element_type=jnp.float32)
        return carry

    lax.fori_loop(0, TP, step, 0)
    for h in range(3):
        cols = slice(h * HD, (h + 1) * HD)
        kv_ref[:, cols] = head_norm(total[:, cols], gain_ref[h : h + 1, :]).astype(jnp.bfloat16)
    kv_ref[:, 384:] = total[:, 384:].astype(jnp.bfloat16)


def project_q_kernel(x_ref, *refs):
    q_parts, gain_ref, q_ref, held, total, sems = refs[:2], refs[2], refs[3], refs[4], refs[5], refs[6]
    both = [(dc, dx, q_parts[dc].at[dx]) for dc in range(2) for dx in range(2)]
    copies = load_weight(both, held, 0, sems, 0)
    for copy in copies:
        copy.start()
    for copy in copies:
        copy.wait()
    total[...] = jnp.zeros_like(total)

    def step(t, carry):
        weight = held[t].reshape(KB, 384)
        total[...] += jnp.dot(x_ref[t], weight, preferred_element_type=jnp.float32)
        return carry

    lax.fori_loop(0, TP, step, 0)
    for h in range(3):
        cols = slice(h * HD, (h + 1) * HD)
        q_ref[:, cols] = head_norm(total[:, cols], gain_ref[h : h + 1, :]).astype(jnp.bfloat16)


VM = pl.BlockSpec(memory_space=pltpu.VMEM)


def project(kernel, normed, parts, gain, width):
    n = len(parts)
    return pl.pallas_call(
        kernel,
        out_shape=jax.ShapeDtypeStruct((512, width), jnp.bfloat16),
        in_specs=[VM] + [ANY] * n + [VM],
        out_specs=VM,
        scratch_shapes=[
            pltpu.VMEM((TP, 2, 2, SUB, width), jnp.bfloat16),
            pltpu.VMEM((512, width), jnp.float32),
            pltpu.SemaphoreType.DMA((32 * (width // 384),)),
        ],
        compiler_params=pltpu.CompilerParams(vmem_limit_bytes=VMEM_LIMIT),
    )(normed, *parts, gain)


def attend_kernel(n_parts, q_ref, *refs):
    parts, outs, held, sems = refs[:n_parts], refs[n_parts : n_parts + 4], refs[-2], refs[-1]
    row = 0
    copies = []
    for i, part in enumerate(parts):
        rows = part.shape[0]
        copies.append(pltpu.make_async_copy(part, held.at[pl.ds(row, rows), :], sems.at[i]))
        row += rows
    for copy in copies:
        copy.start()
    for copy in copies:
        copy.wait()
    scale = 1.0 / (HD ** 0.5)
    for h in range(3):
        for s in range(4):
            q = q_ref[s * 128 : (s + 1) * 128, h * HD : (h + 1) * HD]
            keys = held[:, h * HD : (h + 1) * HD]
            scores = lax.dot_general(
                q, keys, (((1,), (1,)), ((), ())), preferred_element_type=jnp.float32
            ) * scale
            expd = jnp.exp(scores - jnp.max(scores, axis=-1, keepdims=True))
            totals = jnp.sum(expd, axis=-1, keepdims=True)
            values = held[:, 384 + h * HD : 384 + (h + 1) * HD]
            summed = jnp.dot(expd.astype(jnp.bfloat16), values, preferred_element_type=jnp.float32)
            outs[s][:, h * HD : (h + 1) * HD] = (summed / totals).astype(jnp.bfloat16)


def attend(queries, parts):
    n = len(parts)
    return pl.pallas_call(
        lambda *refs: attend_kernel(n, *refs),
        out_shape=[jax.ShapeDtypeStruct((128, 384), jnp.bfloat16)] * 4,
        in_specs=[VM] + [ANY] * n,
        out_specs=[VM] * 4,
        scratch_shapes=[
            pltpu.VMEM((4096, 768), jnp.bfloat16),
            pltpu.SemaphoreType.DMA((n,)),
        ],
        compiler_params=pltpu.CompilerParams(vmem_limit_bytes=VMEM_LIMIT),
    )(queries, *parts)


def shards(patches, ln_gain, w_qkv, query_gain, key_gain):
    zh = lax.axis_index("zh")

    def crop(s):
        return lax.dynamic_index_in_dim(patches, lax.rem(zh + s, 4), 0, keepdims=False)

    def weight(i):
        return w_qkv[:, i].reshape(SUB, 384)

    sent = [lax.ppermute(crop(s), "zh", ring(4, s)) for s in (1, 3, 2)]
    chunks = (crop(0), jnp.concatenate([sent[0], sent[2], sent[1]], axis=0))
    pieces = []
    for chunk in chunks:
        other = lax.ppermute(chunk, "xh", SWAP)
        pair = jnp.stack([chunk, other])
        fwd = lax.ppermute(pair, "y", ring(4, 1))
        bwd = lax.ppermute(pair, "y", ring(4, -1))
        far0 = lax.ppermute(fwd[0], "y", ring(4, 1))
        far1 = lax.ppermute(bwd[1], "y", ring(4, -1))
        pieces += [chunk, other, fwd, bwd, far0, far1]
    wk0 = lax.all_gather(weight(1), ("zh", "zl"), axis=0)
    wk1 = lax.ppermute(wk0, "xl", SWAP)
    wk2 = lax.ppermute(wk0, "core", SWAP)
    wk3 = lax.ppermute(wk1, "core", SWAP)

    def gather_pair(part):
        pair = jnp.stack([part, lax.ppermute(part, "xl", SWAP)])
        own = lax.all_gather(pair, ("zh", "zl"), axis=1)
        return own, lax.ppermute(own, "core", SWAP)

    wv = gather_pair(weight(2))
    wq = gather_pair(weight(0))

    normed = norm_rows(pieces, ln_gain.reshape(TP, KB))
    kv = project(project_kv_kernel, normed, (wk0, wk1, wk2, wk3) + wv, key_gain, 768)
    across_x = lax.ppermute(kv, "xl", SWAP)
    across_z = lax.ppermute(kv, "zl", SWAP)
    queries = project(project_q_kernel, normed, wq, query_gain, 384)
    diag0 = lax.ppermute(across_x[:256], "zl", SWAP)
    diag1 = lax.ppermute(across_z[256:], "xl", SWAP)
    mine = [kv, across_x, across_z, diag0, diag1]
    theirs = [lax.ppermute(part, "core", SWAP) for part in mine]
    outs = attend(queries, mine + theirs)
    back = [outs[0]] + [lax.ppermute(outs[s], "zh", ring(4, -s)) for s in (1, 2, 3)]
    doubled = jnp.stack(back + back)
    ordered = lax.dynamic_slice_in_dim(doubled, 4 - zh, 4, axis=0)
    return ordered.reshape(4, 128, 3, HD)


def solution(mesh):
    fine = Mesh(mesh.devices.reshape(2, 4, 2, 2, 2, 4), ("xl", "zh", "zl", "core", "xh", "y"))
    ctx, tp = ("xl", "zh", "zl", "core"), ("xh", "y")
    return jax.shard_map(
        shards,
        mesh=fine,
        in_specs=(P(None, ctx, tp), P(), P(ctx, None, tp, None), P(tp, None), P(tp, None)),
        out_specs=P(None, ctx, tp, None),
        check_vma=False,
    )
```

```python
import jax
import jax.numpy as jnp
from jax import lax
from jax.experimental import pallas as pl
from jax.experimental.pallas import tpu as pltpu
from jax.sharding import Mesh, PartitionSpec as P

TP = 8
KB = 768
SUB = 192
HD = 128
W = 384
SWAP = [(0, 1), (1, 0)]
VMEM_LIMIT = 58 * 1024 * 1024
ANY = pl.BlockSpec(memory_space=pl.ANY)
VM = pl.BlockSpec(memory_space=pltpu.VMEM)
BF, F32 = jnp.bfloat16, jnp.float32


def ring(n, shift):
    return [(i, (i + shift) % n) for i in range(n)]


def after(value, *others):
    return lax.optimization_barrier((value,) + others)[0]


def call(kernel, outs, ins, scratch, flops, moved):
    return pl.pallas_call(
        kernel,
        out_shape=outs,
        in_specs=ins,
        out_specs=[VM] * len(outs),
        scratch_shapes=scratch,
        cost_estimate=pl.CostEstimate(flops=flops, transcendentals=0, bytes_accessed=moved),
        compiler_params=pltpu.CompilerParams(vmem_limit_bytes=VMEM_LIMIT),
    )


def norm_kernel(c0, c1, f, b, g, h, gain_ref, out_ref, held, sems):
    xh, y = lax.axis_index("xh"), lax.axis_index("y")
    plan = (
        (c0, 0, 0), (c1, 1, 0), (f.at[0], 0, 3), (f.at[1], 1, 3),
        (b.at[0], 0, 1), (b.at[1], 1, 1), (g, 0, 2), (h, 1, 2),
    )
    copies = []
    for src, dx, dy in plan:
        t = lax.rem(xh + dx, 2) * 4 + lax.rem(y + dy, 4)
        copies.append(pltpu.make_async_copy(src, held.at[t], sems.at[len(copies)]))
    for copy in copies:
        copy.start()
    for copy in copies:
        copy.wait()
    tile = 16

    def rows_step(i, carry):
        r = pl.multiple_of(i * tile, tile)
        part = jnp.zeros((tile, 128), F32)
        part2 = jnp.zeros((tile, 128), F32)
        for t in range(TP):
            block = held[t, pl.ds(r, tile), :].astype(F32)
            for j in range(KB // 128):
                piece = block[:, j * 128 : (j + 1) * 128]
                part = part + piece
                part2 = part2 + piece * piece
        center = jnp.sum(part, axis=-1, keepdims=True) * (1.0 / (TP * KB))
        spread = jnp.sum(part2, axis=-1, keepdims=True) * (1.0 / (TP * KB)) - center * center
        scale = lax.rsqrt(spread + 1e-06)
        for t in range(TP):
            xl, zh = t // 4, t % 4
            block = held[t, pl.ds(r, tile), :].astype(F32)
            block = ((block - center) * scale * gain_ref[t : t + 1, :]).astype(BF)
            for zl in range(2):
                out_ref[2 * zh + zl, pl.ds(r, tile), xl * W : (xl + 1) * W] = block[:, zl * W : (zl + 1) * W]
        return carry

    lax.fori_loop(0, held.shape[1] // tile, rows_step, 0)


def norm_rows(pieces, gain):
    rows = pieces[0].shape[0]
    return call(
        norm_kernel,
        [jax.ShapeDtypeStruct((8, rows, KB), BF)],
        [ANY] * 6 + [VM],
        [pltpu.VMEM((TP, rows, KB), BF), pltpu.SemaphoreType.DMA((8,))],
        rows * 6144 * 12,
        rows * 6144 * 4,
    )(*pieces, gain)[0]


def head_norm(values_in, gain):
    center = jnp.mean(values_in, axis=-1, keepdims=True)
    spread = jnp.mean(values_in * values_in, axis=-1, keepdims=True) - center * center
    return (values_in - center) * lax.rsqrt(spread + 1e-06) * gain


def product_call(blocks, normed, begun, arrays, gain, col, width):
    n, m = len(blocks), len(arrays)

    def kernel(x_own, x_rest, *refs):
        refs = list(refs)
        begun_ref = refs.pop(0) if begun is not None else None
        sources, refs = refs[:m], refs[m:]
        gain_ref = refs.pop(0) if gain is not None else None
        out, xbuf, wbuf, sems, sem = refs[0], refs[-4], refs[-3], refs[-2], refs[-1]
        total = out if gain is None else refs[1]
        xl, core = lax.axis_index("xl"), lax.axis_index("core")
        z = 2 * lax.axis_index("zh") + lax.axis_index("zl")
        if begun is not None:
            first = pltpu.make_async_copy(begun_ref.at[:, pl.ds(col, width)], total, sem)
            first.start()

        def weight_copy(source, k, dx, dc):
            return pltpu.make_async_copy(
                source.at[:, pl.ds(col, width)],
                wbuf.at[k, lax.rem(xl + dx, 2), lax.rem(core + dc, 2)],
                sems.at[k, 2 + 2 * dx + dc],
            )

        def rows_copies(at, k):
            return (
                pltpu.make_async_copy(x_own.at[at], xbuf.at[k, 0:128, :], sems.at[k, 0]),
                pltpu.make_async_copy(x_rest.at[at], xbuf.at[k, 128:512, :], sems.at[k, 1]),
            )

        like = None
        for k, (up, down, find) in enumerate(blocks):
            at = lax.rem(z + 8 + up + core * (down - up), 8)
            for copy in rows_copies(at, k):
                copy.start()
            for dx in range(2):
                for dc in range(2):
                    i, index = find(dc, dx)
                    like = sources[i].at[index]
                    weight_copy(like, k, dx, dc).start()
        if begun is None:
            total[...] = jnp.zeros_like(total)
        else:
            first.wait()

        def step(k, carry):
            for copy in rows_copies(0, k):
                copy.wait()
            for dx in range(2):
                for dc in range(2):
                    weight_copy(like, k, dx, dc).wait()
            total[...] += jnp.dot(xbuf[k], wbuf[k].reshape(KB, width), preferred_element_type=F32)
            return carry

        lax.fori_loop(0, n, step, 0)
        if gain is not None:
            for h in range(3):
                cols = slice(h * HD, (h + 1) * HD)
                out[:, cols] = head_norm(total[:, cols], gain_ref[h : h + 1, :]).astype(BF)
            if width > W:
                out[:, W:] = total[:, W:].astype(BF)

    args = [*normed, *(() if begun is None else (begun,)), *arrays, *(() if gain is None else (gain,))]
    return call(
        kernel,
        [jax.ShapeDtypeStruct((512, width), F32 if gain is None else BF)],
        [ANY] * (len(args) - (gain is not None)) + [VM] * (gain is not None),
        ([] if gain is None else [pltpu.VMEM((512, width), F32)])
        + [
            pltpu.VMEM((n, 512, KB), BF),
            pltpu.VMEM((n, 2, 2, SUB, width), BF),
            pltpu.SemaphoreType.DMA((n, 6)),
            pltpu.SemaphoreType.DMA,
        ],
        n * 2 * 512 * KB * width,
        n * (512 * KB + KB * width) * 2 + 512 * width * 8,
    )(*args)[0]


def both_cores(i, s):
    return [
        (-s, s, lambda dc, dx: (i, (dc, dx))),
        (s, -s, lambda dc, dx: (i + 1, (1 - dc, dx))),
    ]


SCALE = 1.0 / (HD ** 0.5)


def attend(queries, state, parts, last):
    n, keys_n = len(parts), sum(part.shape[0] for part in parts)
    begins = state is None

    def kernel(q_ref, *refs):
        refs = list(refs)
        old = None if begins else (refs.pop(0), refs.pop(0))
        sources, refs = refs[:n], refs[n:]
        outs, held, sems = refs[:-2], refs[-2], refs[-1]
        row, copies = 0, []
        for i, source in enumerate(sources):
            rows = source.shape[0]
            copies.append(pltpu.make_async_copy(source, held.at[pl.ds(row, rows), :], sems.at[i]))
            row += rows
        for copy in copies:
            copy.start()
        for copy in copies:
            copy.wait()
        zh = lax.axis_index("zh")
        tile = 256

        def head(h, carry):
            cols = pl.ds(pl.multiple_of(h * HD, HD), HD)
            value_cols = pl.ds(pl.multiple_of(W + h * HD, HD), HD)
            keys, values = held[:, cols], held[:, value_cols]
            for part in range(512 // tile):
                rows = slice(part * tile, part * tile + tile)
                scores = lax.dot_general(
                    q_ref[rows, cols], keys, (((1,), (1,)), ((), ())), preferred_element_type=F32
                ) * SCALE
                best = jnp.max(scores, axis=-1, keepdims=True)
                if not begins:
                    before = old[1][h, rows, 0:1]
                    best = jnp.maximum(best, before)
                expd = jnp.exp(scores - best)
                totals = jnp.sum(expd, axis=-1, keepdims=True)
                summed = jnp.dot(expd.astype(BF), values, preferred_element_type=F32)
                if not begins:
                    keep = jnp.exp(before - best)
                    totals = totals + keep * old[1][h, rows, 1:2]
                    summed = summed + keep * old[0][rows, cols]
                if last:
                    result = (summed / totals).astype(BF)
                    for s in range(part * tile // 128, (part + 1) * tile // 128):
                        here = slice(s * 128 - part * tile, s * 128 + 128 - part * tile)
                        outs[0][lax.rem(zh + s, 4), :, cols] = result[here]
                else:
                    outs[0][rows, cols] = summed
                    outs[1][h, rows, 0:1] = best
                    outs[1][h, rows, 1:2] = totals
            return carry

        lax.fori_loop(0, 3, head, 0)

    if last:
        out_shape = [jax.ShapeDtypeStruct((4, 128, W), BF)]
    else:
        out_shape = [jax.ShapeDtypeStruct((512, W), F32), jax.ShapeDtypeStruct((3, 512, HD), F32)]
    return call(
        kernel,
        out_shape,
        [VM] * (1 if begins else 3) + [ANY] * n,
        [pltpu.VMEM((keys_n, 2 * W), BF), pltpu.SemaphoreType.DMA((n,))],
        512 * keys_n * 3 * HD * 8,
        keys_n * 2 * W * 2 + 512 * W * 8,
    )(queries, *(() if begins else state), *parts)


def shards(patches, ln_gain, w_qkv, query_gain, key_gain):
    zh = lax.axis_index("zh")
    gain = ln_gain.reshape(TP, KB)

    def send(value, axis, n, shift):
        return lax.ppermute(value, axis, ring(n, shift))

    def swap(value, axis):
        return lax.ppermute(value, axis, SWAP)

    both_ways = [(2 * z + c, 2 * ((z + (1, -1)[c]) % 8) + c) for z in range(8) for c in range(2)]

    def send_z(value):
        return lax.ppermute(value, ("zh", "zl", "core"), both_ways)

    weight = w_qkv.reshape(SUB, 3 * W)
    mine = lax.dynamic_index_in_dim(patches, zh, 0, keepdims=False)
    mine_x = swap(mine, "xh")
    weight_x = swap(weight, "xl")
    crops = lax.all_to_all(patches, "zh", 0, 0, tiled=True)
    crops = jnp.concatenate([crops, crops[:3]])
    rest = lax.dynamic_slice_in_dim(crops, zh + 1, 3, axis=0).reshape(384, KB)
    rest_x = swap(rest, "xh")
    w0 = jnp.stack([weight, weight_x])
    w0_c = swap(after(w0, rest), "core")
    mine_pair = after(jnp.stack([mine, mine_x]), rest)
    mine_f, mine_b = send(mine_pair, "y", 4, 1), send(mine_pair, "y", 4, -1)
    w0_both = jnp.stack([w0, w0_c])
    r1 = send_z(w0_both)
    mine_g, mine_h = send(mine_f[0], "y", 4, 1), send(mine_b[1], "y", 4, -1)
    normed_mine = norm_rows((mine, mine_x, mine_f, mine_b, mine_g, mine_h), gain)
    rest_pair = after(jnp.stack([rest, rest_x]), mine_g, mine_h)
    rest_f, rest_b = send(rest_pair, "y", 4, 1), send(rest_pair, "y", 4, -1)
    r1 = after(r1, rest_pair, normed_mine)
    r2, r1_c = send_z(r1), swap(r1, "core")
    rest_g, rest_h = send(rest_f[0], "y", 4, 1), send(rest_b[1], "y", 4, -1)
    r2 = after(r2, r1_c, rest_f, rest_b)
    r3, r2_c = send_z(r2), swap(r2, "core")
    normed_rest = norm_rows((rest, rest_x, rest_f, rest_b, rest_g, rest_h), gain)
    r3 = after(r3, r2_c, normed_rest)
    r4, r3_c = send_z(r3[0]), swap(r3, "core")
    normed = (normed_mine, normed_rest)
    first = [(0, 0, lambda dc, dx: (0, (dc, dx)))] + both_cores(1, 1) + both_cores(3, 2)
    begun = product_call(first, normed, None, (w0_both, r1, r1_c, r2, r2_c), None, 0, 3 * W)
    begun = product_call(both_cores(0, 3), normed, after(begun, r3_c), (r3, r3_c), None, 0, 3 * W)
    r4 = after(r4, begun)
    r4_c = swap(r4, "core")
    final = [(4, 4, lambda dc, dx: (dc, dx))]
    near = product_call(final, normed, begun, (r4, r4_c), key_gain, W, 2 * W)

    across_x, across_z, near_c = swap(near, "xl"), swap(near, "zl"), swap(near, "core")
    queries = product_call(final, normed, begun, (r4, r4_c), query_gain, 0, W)
    state = attend(queries, None, (near, near_c), False)
    across_x, across_z = after(across_x, state[1]), after(across_z, state[1])
    diag0, diag1 = swap(across_x[:256], "zl"), swap(across_z[256:], "xl")
    across_x_c, across_z_c = swap(across_x, "core"), swap(across_z, "core")
    state = attend(queries, state, (across_x, across_z, across_x_c, across_z_c), False)
    diag0, diag1 = after(diag0, state[1]), after(diag1, state[1])
    diag0_c, diag1_c = swap(diag0, "core"), swap(diag1, "core")
    (out,) = attend(queries, state, (diag0, diag1, diag0_c, diag1_c), True)
    out = lax.all_to_all(out, "zh", 0, 0, tiled=True)
    return out.reshape(4, 128, 3, HD)


def solution(mesh):
    fine = Mesh(mesh.devices.reshape(2, 4, 2, 2, 2, 4), ("xl", "zh", "zl", "core", "xh", "y"))
    ctx, tp = ("xl", "zh", "zl", "core"), ("xh", "y")
    return jax.shard_map(
        shards,
        mesh=fine,
        in_specs=(P(None, ctx, tp), P(), P(ctx, None, tp, None), P(tp, None), P(tp, None)),
        out_specs=P(None, ctx, tp, None),
        check_vma=False,
    )
```

```python
import jax
import jax.numpy as jnp
from jax import lax
from jax.experimental import pallas as pl
from jax.experimental.pallas import tpu as pltpu
from jax.sharding import Mesh, PartitionSpec as P

TP = 8
KB = 768
SUB = 192
HD = 128
W = 384
SWAP = [(0, 1), (1, 0)]
VMEM_LIMIT = 58 * 1024 * 1024
ANY = pl.BlockSpec(memory_space=pl.ANY)
VM = pl.BlockSpec(memory_space=pltpu.VMEM)
BF, F32 = jnp.bfloat16, jnp.float32


def ring(n, shift):
    return [(i, (i + shift) % n) for i in range(n)]


def after(value, *others):
    return lax.optimization_barrier((value,) + others)[0]


def call(kernel, outs, ins, scratch, flops, moved):
    return pl.pallas_call(
        kernel,
        out_shape=outs,
        in_specs=ins,
        out_specs=[VM] * len(outs),
        scratch_shapes=scratch,
        cost_estimate=pl.CostEstimate(flops=flops, transcendentals=0, bytes_accessed=moved),
        compiler_params=pltpu.CompilerParams(vmem_limit_bytes=VMEM_LIMIT),
    )


def norm_kernel(c0, c1, f0, f1, b0, b1, g0, g1, h0, h1, gain_ref, out_ref, held, sems):
    xh, y = lax.axis_index("xh"), lax.axis_index("y")
    half = g0.shape[0]
    plan = (
        (c0, 0, 0, 0), (c1, 1, 0, 0), (f0, 0, 3, 0), (f1, 1, 3, 0), (b0, 0, 1, 0), (b1, 1, 1, 0),
        (g0, 0, 2, 0), (g1, 1, 2, 0), (h0, 0, 2, half), (h1, 1, 2, half),
    )
    copies = []
    for src, dx, dy, row in plan:
        t = lax.rem(xh + dx, 2) * 4 + lax.rem(y + dy, 4)
        copies.append(
            pltpu.make_async_copy(src, held.at[t, pl.ds(row, src.shape[0]), :], sems.at[len(copies)])
        )
    for copy in copies:
        copy.start()
    for copy in copies:
        copy.wait()
    tile = 32

    def rows_step(i, carry):
        r = pl.multiple_of(i * tile, tile)
        part = jnp.zeros((tile, 128), F32)
        part2 = jnp.zeros((tile, 128), F32)
        for t in range(TP):
            for j in range(KB // 128):
                piece = held[t, pl.ds(r, tile), j * 128 : (j + 1) * 128].astype(F32)
                part = part + piece
                part2 = part2 + piece * piece
        center = jnp.sum(part, axis=-1, keepdims=True) * (1.0 / (TP * KB))
        spread = jnp.sum(part2, axis=-1, keepdims=True) * (1.0 / (TP * KB)) - center * center
        scale = jnp.broadcast_to(lax.rsqrt(spread + 1e-06), (tile, 128))
        center = jnp.broadcast_to(center, (tile, 128))
        for t in range(TP):
            xl, zh = t // 4, t % 4
            for j in range(KB // 128):
                piece = held[t, pl.ds(r, tile), j * 128 : (j + 1) * 128].astype(F32)
                piece = ((piece - center) * scale * gain_ref[t : t + 1, j * 128 : (j + 1) * 128]).astype(BF)
                zl, k = j // 3, j % 3
                out_ref[2 * zh + zl, pl.ds(r, tile), xl * W + k * 128 : xl * W + (k + 1) * 128] = piece
        return carry

    lax.fori_loop(0, held.shape[1] // tile, rows_step, 0)


def norm_rows(pieces, gain):
    rows = pieces[0].shape[0]
    return call(
        norm_kernel,
        [jax.ShapeDtypeStruct((8, rows, KB), BF)],
        [ANY] * 10 + [VM],
        [pltpu.VMEM((TP, rows, KB), BF), pltpu.SemaphoreType.DMA((10,))],
        rows * 6144 * 12,
        rows * 6144 * 4,
    )(*pieces, gain)[0]


def head_norm(values_in, gain):
    center = jnp.mean(values_in, axis=-1, keepdims=True)
    spread = jnp.mean(values_in * values_in, axis=-1, keepdims=True) - center * center
    return (values_in - center) * lax.rsqrt(spread + 1e-06) * gain


def product_call(blocks, normed, begun, arrays, gain, col, width):
    n, m = len(blocks), len(arrays)

    def kernel(x_own, x_rest, *refs):
        refs = list(refs)
        begun_ref = refs.pop(0) if begun is not None else None
        sources, refs = refs[:m], refs[m:]
        gain_ref = refs.pop(0) if gain is not None else None
        out, xbuf, wbuf, sems, sem = refs[0], refs[-4], refs[-3], refs[-2], refs[-1]
        total = out if gain is None else refs[1]
        xl, core = lax.axis_index("xl"), lax.axis_index("core")
        z = 2 * lax.axis_index("zh") + lax.axis_index("zl")
        if begun is not None:
            first = pltpu.make_async_copy(begun_ref.at[:, pl.ds(col, width)], total, sem)
            first.start()

        def weight_copy(source, k, dx, dc):
            return pltpu.make_async_copy(
                source.at[:, pl.ds(col, width)],
                wbuf.at[k, lax.rem(xl + dx, 2), lax.rem(core + dc, 2)],
                sems.at[k, 2 + 2 * dx + dc],
            )

        def rows_copies(at, k):
            return (
                pltpu.make_async_copy(x_own.at[at], xbuf.at[k, 0:128, :], sems.at[k, 0]),
                pltpu.make_async_copy(x_rest.at[at], xbuf.at[k, 128:512, :], sems.at[k, 1]),
            )

        like = None
        for k, (up, down, find) in enumerate(blocks):
            at = lax.rem(z + 8 + up + core * (down - up), 8)
            for copy in rows_copies(at, k):
                copy.start()
            for dx in range(2):
                for dc in range(2):
                    i, index = find(dc, dx)
                    like = sources[i].at[index]
                    weight_copy(like, k, dx, dc).start()
        if begun is None:
            total[...] = jnp.zeros_like(total)
        else:
            first.wait()

        def step(k, carry):
            for copy in rows_copies(0, k):
                copy.wait()
            for dx in range(2):
                for dc in range(2):
                    weight_copy(like, k, dx, dc).wait()
            total[...] += jnp.dot(xbuf[k], wbuf[k].reshape(KB, width), preferred_element_type=F32)
            return carry

        lax.fori_loop(0, n, step, 0)
        if gain is not None:
            for h in range(3):
                cols = slice(h * HD, (h + 1) * HD)
                out[:, cols] = head_norm(total[:, cols], gain_ref[h : h + 1, :]).astype(BF)
            if width > W:
                out[:, W:] = total[:, W:].astype(BF)

    args = [*normed, *(() if begun is None else (begun,)), *arrays, *(() if gain is None else (gain,))]
    return call(
        kernel,
        [jax.ShapeDtypeStruct((512, width), F32 if gain is None else BF)],
        [ANY] * (len(args) - (gain is not None)) + [VM] * (gain is not None),
        ([] if gain is None else [pltpu.VMEM((512, width), F32)])
        + [
            pltpu.VMEM((n, 512, KB), BF),
            pltpu.VMEM((n, 2, 2, SUB, width), BF),
            pltpu.SemaphoreType.DMA((n, 6)),
            pltpu.SemaphoreType.DMA,
        ],
        n * 2 * 512 * KB * width,
        n * (512 * KB + KB * width) * 2 + 512 * width * 8,
    )(*args)[0]


def both_cores(i, s):
    return [
        (-s, s, lambda dc, dx: (i, (dc, dx))),
        (s, -s, lambda dc, dx: (i + 1, (1 - dc, dx))),
    ]


SCALE = 1.4426950408889634 / (HD ** 0.5)


def attend(queries, state, parts, blocks, last):
    n, keys_n = len(parts), sum(part.shape[0] for part in parts)
    begins = state is None

    def kernel(q_ref, *refs):
        refs = list(refs)
        old = None if begins else (refs.pop(0), refs.pop(0))
        sources, refs = refs[:n], refs[n:]
        outs, held, sems = refs[:-2], refs[-2], refs[-1]
        row, copies = 0, []
        for i, source in enumerate(sources):
            rows = source.shape[0]
            copies.append(pltpu.make_async_copy(source, held.at[pl.ds(row, rows), :], sems.at[i]))
            row += rows
        for copy in copies:
            copy.start()
        for copy in copies:
            copy.wait()
        for h in range(3):
            cols = slice(h * HD, (h + 1) * HD)
            keys, values = held[:, cols], held[:, W + h * HD : W + (h + 1) * HD]
            for first, size in blocks:
                rows = slice(first * 128, (first + size) * 128)
                scores = lax.dot_general(
                    q_ref[rows, cols], keys, (((1,), (1,)), ((), ())), preferred_element_type=F32
                )
                best = jnp.max(scores, axis=-1, keepdims=True)
                if not begins:
                    before = old[1][h, rows, 0:1]
                    best = jnp.maximum(best, before)
                expd = jnp.exp2((scores - best) * SCALE)
                totals = jnp.sum(expd, axis=-1, keepdims=True)
                summed = jnp.dot(expd.astype(BF), values, preferred_element_type=F32)
                if not begins:
                    keep = jnp.exp2((before - best) * SCALE)
                    totals = totals + keep * old[1][h, rows, 1:2]
                    summed = summed + keep * old[0][rows, cols]
                if last:
                    result = (summed / totals).astype(BF)
                    for s in range(size):
                        out = outs[[b for f, z in blocks for b in range(f, f + z)].index(first + s)]
                        out[h] = result[s * 128 : (s + 1) * 128]
                else:
                    outs[0][rows, cols] = summed
                    outs[1][h, rows, 0:1] = best
                    outs[1][h, rows, 1:2] = totals

    if last:
        out_shape = [jax.ShapeDtypeStruct((3, 128, HD), BF)] * sum(size for _, size in blocks)
    else:
        out_shape = [jax.ShapeDtypeStruct((512, W), F32), jax.ShapeDtypeStruct((3, 512, HD), F32)]
    return call(
        kernel,
        out_shape,
        [VM] * (1 if begins else 3) + [ANY] * n,
        [pltpu.VMEM((keys_n, 2 * W), BF), pltpu.SemaphoreType.DMA((n,))],
        512 * keys_n * 3 * HD * 8,
        keys_n * 2 * W * 2 + 512 * W * 8,
    )(queries, *(() if begins else state), *parts)


def place_crops(parts):
    def kernel(*refs):
        out, sems = refs[4], refs[5]
        zh = lax.axis_index("zh")
        copies = [
            pltpu.make_async_copy(refs[s], out.at[lax.rem(zh + 4 - s, 4)], sems.at[s]) for s in range(4)
        ]
        for copy in copies:
            copy.start()
        for copy in copies:
            copy.wait()

    return call(
        kernel,
        [jax.ShapeDtypeStruct((4, 3, 128, HD), BF)],
        [ANY] * 4,
        [pltpu.SemaphoreType.DMA((4,))],
        0,
        4 * 128 * W * 4,
    )(*parts)[0]


def shards(patches, ln_gain, w_qkv, query_gain, key_gain):
    zh = lax.axis_index("zh")
    gain = ln_gain.reshape(TP, KB)

    def send(value, axis, n, shift):
        return lax.ppermute(value, axis, ring(n, shift))

    def swap(value, axis):
        return lax.ppermute(value, axis, SWAP)

    both_ways = [(2 * z + c, 2 * ((z + (1, -1)[c]) % 8) + c) for z in range(8) for c in range(2)]

    def send_z(value):
        return lax.ppermute(value, ("zh", "zl", "core"), both_ways)

    weight = w_qkv.reshape(SUB, 3 * W)
    crops = lax.all_to_all(patches, "zh", 0, 0, tiled=True)
    mine = lax.dynamic_index_in_dim(patches, zh, 0, keepdims=False)
    mine_x = swap(mine, "xh")
    weight_x = swap(weight, "xl")
    mine_pair = jnp.stack([mine, mine_x])
    mine_f, mine_b = send(mine_pair, "y", 4, 1), send(mine_pair, "y", 4, -1)
    w0 = jnp.stack([weight, weight_x])
    w0_both = jnp.stack([w0, swap(after(w0, mine_pair), "core")])
    mine_g, mine_h = send(mine_f[:, :64], "y", 4, 1), send(mine_b[:, 64:], "y", 4, -1)
    crops = after(crops, mine_x, weight_x)
    crops = jnp.concatenate([crops, crops[:3]])
    rest = lax.dynamic_slice_in_dim(crops, zh + 1, 3, axis=0).reshape(384, KB)
    rest_x = swap(rest, "xh")
    r1 = send_z(after(w0_both, rest, mine_f, mine_b))
    rest_f, rest_b = send(rest, "y", 4, 1), send(rest, "y", 4, -1)
    normed_mine = norm_rows(
        (mine, mine_x, mine_f[0], mine_f[1], mine_b[0], mine_b[1], mine_g[0], mine_g[1], mine_h[0], mine_h[1]), gain
    )
    rest_x = after(rest_x, normed_mine)
    far_f, far_b = send(rest_x, "y", 4, 1), send(rest_x, "y", 4, -1)
    rest_g, rest_h = send(rest_f[:192], "y", 4, 1), send(rest_b[192:], "y", 4, -1)
    r1 = after(r1, rest_x, rest_f, rest_b)
    r2, r1_c = send_z(r1), swap(r1, "core")
    far_g, far_h = send(far_f[:192], "y", 4, 1), send(far_b[192:], "y", 4, -1)
    r2 = after(r2, r1_c, far_f, far_b, rest_g, rest_h)
    r3, r2_c = send_z(r2), swap(r2, "core")
    normed_rest = norm_rows(
        (rest, rest_x, rest_f, far_f, rest_b, far_b, rest_g, far_g, rest_h, after(far_h, r2)), gain
    )
    r3 = after(r3, r2_c, normed_rest)
    r4, r3_c = send_z(r3[0]), swap(r3, "core")
    normed = (normed_mine, normed_rest)
    first = [(0, 0, lambda dc, dx: (0, (dc, dx)))] + both_cores(1, 1) + both_cores(3, 2)
    begun = product_call(first, normed, None, (w0_both, r1, r1_c, r2, r2_c), None, 0, 3 * W)
    begun = product_call(both_cores(0, 3), normed, after(begun, r3_c), (r3, r3_c), None, 0, 3 * W)
    r4 = after(r4, begun)
    r4_c = swap(r4, "core")
    final = [(4, 4, lambda dc, dx: (dc, dx))]
    near = product_call(final, normed, begun, (r4, r4_c), key_gain, W, 2 * W)

    across_x, across_z, near_c = swap(near, "xl"), swap(near, "zl"), swap(near, "core")
    queries = product_call(final, normed, begun, (r4, r4_c), query_gain, 0, W)
    all_rows = [(0, 2), (2, 2)]
    state = attend(queries, None, (near, near_c), all_rows, False)
    across_x, across_z = after(across_x, state[1]), after(across_z, state[1])
    diag0, diag1 = swap(across_x[:256], "zl"), swap(across_z[256:], "xl")
    across_x_c, across_z_c = swap(across_x, "core"), swap(across_z, "core")
    state = attend(queries, state, (across_x, across_z, across_x_c, across_z_c), all_rows, False)
    diag0, diag1 = after(diag0, state[1]), after(diag1, state[1])
    diag0_c, diag1_c = swap(diag0, "core"), swap(diag1, "core")
    parts = (diag0, diag1, diag0_c, diag1_c)
    out1, out2 = attend(queries, state, parts, [(1, 2)], True)
    out0, out3 = attend(after(queries, out2), state, parts, [(0, 1), (3, 1)], True)
    back = (out0, send(out1, "zh", 4, 1), send(out2, "zh", 4, 2), send(out3, "zh", 4, 3))
    return jnp.transpose(place_crops(back), (0, 2, 1, 3))


def solution(mesh):
    fine = Mesh(mesh.devices.reshape(2, 4, 2, 2, 2, 4), ("xl", "zh", "zl", "core", "xh", "y"))
    ctx, tp = ("xl", "zh", "zl", "core"), ("xh", "y")
    return jax.shard_map(
        shards,
        mesh=fine,
        in_specs=(P(None, ctx, tp), P(), P(ctx, None, tp, None), P(tp, None), P(tp, None)),
        out_specs=P(None, ctx, tp, None),
        check_vma=False,
    )
```

```python
import jax
import jax.numpy as jnp
from jax import lax
from jax.experimental import pallas as pl
from jax.experimental.pallas import tpu as pltpu
from jax.sharding import Mesh, PartitionSpec as P

TP = 8
KB = 768
SUB = 192
HD = 128
W = 384
SWAP = [(0, 1), (1, 0)]
VMEM_LIMIT = 58 * 1024 * 1024
ANY = pl.BlockSpec(memory_space=pl.ANY)
VM = pl.BlockSpec(memory_space=pltpu.VMEM)
BF, F32 = jnp.bfloat16, jnp.float32


def ring(n, shift):
    return [(i, (i + shift) % n) for i in range(n)]


def after(value, *others):
    return lax.optimization_barrier((value,) + others)[0]


def call(kernel, outs, ins, scratch, flops, moved):
    return pl.pallas_call(
        kernel,
        out_shape=outs,
        in_specs=ins,
        out_specs=[VM] * len(outs),
        scratch_shapes=scratch,
        cost_estimate=pl.CostEstimate(flops=flops, transcendentals=0, bytes_accessed=moved),
        compiler_params=pltpu.CompilerParams(vmem_limit_bytes=VMEM_LIMIT),
    )


def norm_kernel(c0, c1, f0, f1, b0, b1, g0, g1, h0, h1, gain_ref, out_ref, held, sems):
    xh, y = lax.axis_index("xh"), lax.axis_index("y")
    half = g0.shape[0]
    plan = (
        (c0, 0, 0, 0), (c1, 1, 0, 0), (f0, 0, 3, 0), (f1, 1, 3, 0), (b0, 0, 1, 0), (b1, 1, 1, 0),
        (g0, 0, 2, 0), (g1, 1, 2, 0), (h0, 0, 2, half), (h1, 1, 2, half),
    )
    copies = []
    for src, dx, dy, row in plan:
        t = lax.rem(xh + dx, 2) * 4 + lax.rem(y + dy, 4)
        copies.append(
            pltpu.make_async_copy(src, held.at[t, pl.ds(row, src.shape[0]), :], sems.at[len(copies)])
        )
    for copy in copies:
        copy.start()
    for copy in copies:
        copy.wait()
    tile = 32

    def rows_step(i, carry):
        r = pl.multiple_of(i * tile, tile)
        part = jnp.zeros((tile, 128), F32)
        part2 = jnp.zeros((tile, 128), F32)
        for t in range(TP):
            for j in range(KB // 128):
                piece = held[t, pl.ds(r, tile), j * 128 : (j + 1) * 128].astype(F32)
                part = part + piece
                part2 = part2 + piece * piece
        center = jnp.sum(part, axis=-1, keepdims=True) * (1.0 / (TP * KB))
        spread = jnp.sum(part2, axis=-1, keepdims=True) * (1.0 / (TP * KB)) - center * center
        scale = jnp.broadcast_to(lax.rsqrt(spread + 1e-06), (tile, 128))
        center = jnp.broadcast_to(center, (tile, 128))
        for t in range(TP):
            xl, zh = t // 4, t % 4
            for j in range(KB // 128):
                piece = held[t, pl.ds(r, tile), j * 128 : (j + 1) * 128].astype(F32)
                piece = ((piece - center) * scale * gain_ref[t : t + 1, j * 128 : (j + 1) * 128]).astype(BF)
                zl, k = j // 3, j % 3
                out_ref[2 * zh + zl, pl.ds(r, tile), xl * W + k * 128 : xl * W + (k + 1) * 128] = piece
        return carry

    lax.fori_loop(0, held.shape[1] // tile, rows_step, 0)


def norm_rows(pieces, gain):
    rows = pieces[0].shape[0]
    return call(
        norm_kernel,
        [jax.ShapeDtypeStruct((8, rows, KB), BF)],
        [ANY] * 10 + [VM],
        [pltpu.VMEM((TP, rows, KB), BF), pltpu.SemaphoreType.DMA((10,))],
        rows * 6144 * 12,
        rows * 6144 * 4,
    )(*pieces, gain)[0]


def head_norm(values_in, gain):
    center = jnp.mean(values_in, axis=-1, keepdims=True)
    spread = jnp.mean(values_in * values_in, axis=-1, keepdims=True) - center * center
    return (values_in - center) * lax.rsqrt(spread + 1e-06) * gain


def product_call(blocks, normed, begun, arrays, gain, col, width):
    n, m = len(blocks), len(arrays)

    def kernel(x_ref, *refs):
        refs = list(refs)
        begun_ref = refs.pop(0) if begun is not None else None
        sources, refs = refs[:m], refs[m:]
        gain_ref = refs.pop(0) if gain is not None else None
        out, xbuf, wbuf, sems, sem = refs[0], refs[-4], refs[-3], refs[-2], refs[-1]
        total = out if gain is None else refs[1]
        xl, core = lax.axis_index("xl"), lax.axis_index("core")
        z = 2 * lax.axis_index("zh") + lax.axis_index("zl")
        if begun is not None:
            first = pltpu.make_async_copy(begun_ref.at[:, pl.ds(col, width)], total, sem)
            first.start()

        def weight_copy(source, k, dx, dc):
            return pltpu.make_async_copy(
                source.at[:, pl.ds(col, width)],
                wbuf.at[k, lax.rem(xl + dx, 2), lax.rem(core + dc, 2)],
                sems.at[k, 1 + 2 * dx + dc],
            )

        def rows_copy(at, k):
            return pltpu.make_async_copy(x_ref.at[at], xbuf.at[k], sems.at[k, 0])

        like = None
        for k, (up, down, find) in enumerate(blocks):
            at = lax.rem(z + 8 + up + core * (down - up), 8)
            rows_copy(at, k).start()
            for dx in range(2):
                for dc in range(2):
                    i, index = find(dc, dx)
                    like = sources[i].at[index]
                    weight_copy(like, k, dx, dc).start()
        if begun is None:
            total[...] = jnp.zeros_like(total)
        else:
            first.wait()

        def step(k, carry):
            rows_copy(0, k).wait()
            for dx in range(2):
                for dc in range(2):
                    weight_copy(like, k, dx, dc).wait()
            total[...] += jnp.dot(xbuf[k], wbuf[k].reshape(KB, width), preferred_element_type=F32)
            return carry

        lax.fori_loop(0, n, step, 0)
        if gain is not None:
            for h in range(3):
                cols = slice(h * HD, (h + 1) * HD)
                out[:, cols] = head_norm(total[:, cols], gain_ref[h : h + 1, :]).astype(BF)
            if width > W:
                out[:, W:] = total[:, W:].astype(BF)

    args = [normed, *(() if begun is None else (begun,)), *arrays, *(() if gain is None else (gain,))]
    return call(
        kernel,
        [jax.ShapeDtypeStruct((512, width), F32 if gain is None else BF)],
        [ANY] * (len(args) - (gain is not None)) + [VM] * (gain is not None),
        ([] if gain is None else [pltpu.VMEM((512, width), F32)])
        + [
            pltpu.VMEM((n, 512, KB), BF),
            pltpu.VMEM((n, 2, 2, SUB, width), BF),
            pltpu.SemaphoreType.DMA((n, 5)),
            pltpu.SemaphoreType.DMA,
        ],
        n * 2 * 512 * KB * width,
        n * (512 * KB + KB * width) * 2 + 512 * width * 8,
    )(*args)[0]


def both_cores(i, s):
    return [
        (-s, s, lambda dc, dx: (i, (dc, dx))),
        (s, -s, lambda dc, dx: (i + 1, (1 - dc, dx))),
    ]


SCALE = 1.4426950408889634 / (HD ** 0.5)


def attend(queries, state, parts, blocks, last):
    n, keys_n = len(parts), sum(part.shape[0] for part in parts)
    begins = state is None

    def kernel(q_ref, *refs):
        refs = list(refs)
        old = None if begins else (refs.pop(0), refs.pop(0))
        sources, refs = refs[:n], refs[n:]
        outs, held, sems = refs[:-2], refs[-2], refs[-1]
        row, copies = 0, []
        for i, source in enumerate(sources):
            rows = source.shape[0]
            copies.append(pltpu.make_async_copy(source, held.at[pl.ds(row, rows), :], sems.at[i]))
            row += rows
        for copy in copies:
            copy.start()
        for copy in copies:
            copy.wait()
        for h in range(3):
            cols = slice(h * HD, (h + 1) * HD)
            keys, values = held[:, cols], held[:, W + h * HD : W + (h + 1) * HD]
            for n_block, block in enumerate(blocks):
                if last:
                    rows = pl.ds(pl.multiple_of(lax.rem(lax.axis_index("zh") + block, 4) * 128, 128), 128)
                else:
                    rows = slice(block * 256, block * 256 + 256)
                scores = lax.dot_general(
                    q_ref[rows, cols], keys, (((1,), (1,)), ((), ())), preferred_element_type=F32
                )
                best = jnp.max(scores, axis=-1, keepdims=True)
                if not begins:
                    before = old[1][h, rows, 0:1]
                    best = jnp.maximum(best, before)
                expd = jnp.exp2((scores - best) * SCALE)
                totals = jnp.sum(expd, axis=-1, keepdims=True)
                summed = jnp.dot(expd.astype(BF), values, preferred_element_type=F32)
                if not begins:
                    keep = jnp.exp2((before - best) * SCALE)
                    totals = totals + keep * old[1][h, rows, 1:2]
                    summed = summed + keep * old[0][rows, cols]
                if last:
                    outs[n_block][h] = (summed / totals).astype(BF)
                else:
                    outs[0][rows, cols] = summed
                    outs[1][h, rows, 0:1] = best
                    outs[1][h, rows, 1:2] = totals

    if last:
        out_shape = [jax.ShapeDtypeStruct((3, 128, HD), BF)] * len(blocks)
    else:
        out_shape = [jax.ShapeDtypeStruct((512, W), F32), jax.ShapeDtypeStruct((3, 512, HD), F32)]
    return call(
        kernel,
        out_shape,
        [VM] * (1 if begins else 3) + [ANY] * n,
        [pltpu.VMEM((keys_n, 2 * W), BF), pltpu.SemaphoreType.DMA((n,))],
        512 * keys_n * 3 * HD * 8,
        keys_n * 2 * W * 2 + 512 * W * 8,
    )(queries, *(() if begins else state), *parts)


def place_crops(parts):
    def kernel(*refs):
        out, sems = refs[4], refs[5]
        zh = lax.axis_index("zh")
        copies = [
            pltpu.make_async_copy(refs[s], out.at[lax.rem(zh + 4 - s, 4)], sems.at[s]) for s in range(4)
        ]
        for copy in copies:
            copy.start()
        for copy in copies:
            copy.wait()

    return call(
        kernel,
        [jax.ShapeDtypeStruct((4, 3, 128, HD), BF)],
        [ANY] * 4,
        [pltpu.SemaphoreType.DMA((4,))],
        0,
        4 * 128 * W * 4,
    )(*parts)[0]


def shards(patches, ln_gain, w_qkv, query_gain, key_gain):
    zh = lax.axis_index("zh")
    gain = ln_gain.reshape(TP, KB)

    def send(value, axis, n, shift):
        return lax.ppermute(value, axis, ring(n, shift))

    def swap(value, axis):
        return lax.ppermute(value, axis, SWAP)

    both_ways = [(2 * z + c, 2 * ((z + (1, -1)[c]) % 8) + c) for z in range(8) for c in range(2)]

    def send_z(value):
        return lax.ppermute(value, ("zh", "zl", "core"), both_ways)

    weight = w_qkv.reshape(SUB, 3 * W)
    crops = lax.all_to_all(patches, "zh", 0, 0, tiled=True)
    weight_x = swap(weight, "xl")
    crops = after(crops, weight_x).reshape(512, KB)
    w0 = jnp.stack([weight, weight_x])
    w0_both = jnp.stack([w0, swap(w0, "core")])
    crops_x = swap(crops, "xh")
    near_f, near_b = send(crops, "y", 4, 1), send(crops, "y", 4, -1)
    r1 = send_z(after(w0_both, crops))
    far_f, far_b = send(crops_x, "y", 4, 1), send(crops_x, "y", 4, -1)
    r1 = after(r1, crops_x, near_f, near_b)
    r2, r1_c = send_z(r1), swap(r1, "core")
    near_g, near_h = send(near_f[:256], "y", 4, 1), send(near_b[256:], "y", 4, -1)
    far_g, far_h = send(far_f[:256], "y", 4, 1), send(far_b[256:], "y", 4, -1)
    r2 = after(r2, r1_c, far_f, far_b)
    r3, r2_c = send_z(r2), swap(r2, "core")
    normed = norm_rows(
        (crops, crops_x, near_f, far_f, near_b, far_b, near_g, far_g, near_h, after(far_h, r2)), gain
    )
    r3 = after(r3, r2_c, normed)
    r4, r3_c = send_z(r3[0]), swap(r3, "core")
    first = [(0, 0, lambda dc, dx: (0, (dc, dx)))] + both_cores(1, 1) + both_cores(3, 2)
    begun = product_call(first, normed, None, (w0_both, r1, r1_c, r2, r2_c), None, 0, 3 * W)
    r4 = after(r4, begun)
    r4_c = swap(r4, "core")
    begun = product_call(both_cores(0, 3), normed, after(begun, r3_c), (r3, r3_c), None, 0, 3 * W)
    final = [(4, 4, lambda dc, dx: (dc, dx))]
    near = product_call(final, normed, begun, (r4, r4_c), key_gain, W, 2 * W)

    across_x, across_z, near_c = swap(near, "xl"), swap(near, "zl"), swap(near, "core")
    queries = product_call(final, normed, begun, (r4, r4_c), query_gain, 0, W)
    state = attend(queries, None, (near, near_c), [0, 1], False)
    across_x, across_z = after(across_x, state[1]), after(across_z, state[1])
    diag0, diag1 = swap(across_x[:256], "zl"), swap(across_z[256:], "xl")
    across_x_c, across_z_c = swap(across_x, "core"), swap(across_z, "core")
    state = attend(queries, state, (across_x, across_z, across_x_c, across_z_c), [0, 1], False)
    diag0, diag1 = after(diag0, state[1]), after(diag1, state[1])
    parts = (diag0, diag1, swap(diag0, "core"), swap(diag1, "core"))
    out2, out1, out3 = attend(queries, state, parts, [2, 1, 3], True)
    (out0,) = attend(after(queries, out2), state, parts, [0], True)
    back = (out0, send(out1, "zh", 4, 1), send(out2, "zh", 4, 2), send(out3, "zh", 4, 3))
    return jnp.transpose(place_crops(back), (0, 2, 1, 3))


def solution(mesh):
    fine = Mesh(mesh.devices.reshape(2, 4, 2, 2, 2, 4), ("xl", "zh", "zl", "core", "xh", "y"))
    ctx, tp = ("xl", "zh", "zl", "core"), ("xh", "y")
    return jax.shard_map(
        shards,
        mesh=fine,
        in_specs=(P(None, ctx, tp), P(), P(ctx, None, tp, None), P(tp, None), P(tp, None)),
        out_specs=P(None, ctx, tp, None),
        check_vma=False,
    )
```
